512 devices in a mesh: freq: 64 (over y, x, z_hi, core), blk: 8 (over z_lo).
Axes of the slice: x: 4, y: 4, z: 16 (z_hi: 2, z_lo: 8; z = z_hi * 8 + z_lo), core: 2. Of those that a mesh axis runs over, the one named last changes fastest.
Arguments:
- samples: bfloat16 [1024, 267776], P(('blk', 'freq')), may hold values from -127 to 127, as said below
- slot_order: int32 [8, 128], P('blk'), may hold values from 0 to 127, each once within a row
- flags: int32 [1024], P(('blk', 'freq')), may hold values 0 or 1
Outputs:
- visibilities: float32 [256, 2, 1024, 1024], P('freq', None, 'blk')
The draws below stay inside these ranges and needn't reach their ends.
Inputs may be any that keep to these rules, and one draw needn't show every extreme that they name: `samples`: every sample is a whole number.
All inputs are finite; a program needn't handle non-finite values. No bound on the sum of `flags` on one device may be relied on, other than what follows from the above.
Results may differ from the reference program's by a relative error of at most 0.0059.
Values may be sent and summed in bfloat16 or wider, within the bound.
A program may use at most 64 MiB of HBM per device.

```python
import math
import jax
import jax.numpy as jnp
from jax import lax

CH = 256
TAPS = 12
SPEC = 512
NIN = 1024
NSAMP = 267776
NBLOCKS = 8
BLOCK = 128


def draw_samples(key, part):
    key_amp, key_noise, key_sign = jax.random.split(key, 3)
    count = (SPEC + TAPS - 1) * 2 * CH
    amplitude = jax.random.randint(key_amp, (NIN, 1), 5, 57)
    raw_bits = jax.random.randint(key_noise, (NIN, count + 1), 0, 65536)
    noise = raw_bits % (2 * amplitude + 1) - amplitude
    polarity = jax.random.randint(key_sign, (NIN, 1), 0, 2) * 2 - 1
    values = noise[:, 1:] + polarity * (noise[:, :-1] // 2)
    return values.astype(jnp.float32).astype(jnp.bfloat16)


def place_ends(array, own_key, smallest, high):
    index_at = [jax.random.randint(jax.random.fold_in(own_key, axis), (), 0, length) for axis, length in enumerate(array.shape)]
    widest = array.shape.index(max(array.shape))
    next_to = index_at[:widest] + [(index_at[widest] + 1) % array.shape[widest]] + index_at[widest + 1:]
    return array.at[tuple(index_at)].set(smallest).at[tuple(next_to)].set(high)


def setup_inputs(seed: int = 0) -> dict:
    streams_of = jax.random.split(jax.random.key(seed), 4)
    return {
        "samples": draw_samples(jax.random.fold_in(streams_of[3], 71), 0),
        "slot_order": jax.vmap(lambda own: jax.random.permutation(own, BLOCK))(jax.random.split(streams_of[1], NBLOCKS)).reshape((NBLOCKS, BLOCK)).astype(jnp.int32),
        "flags": place_ends((jax.random.randint(streams_of[2], (NIN,), 0, 8) < 1).astype(jnp.int32), jax.random.fold_in(streams_of[2], 1), 0, 1),
    }


def prototype():
    count = TAPS * 2 * CH
    index = jnp.arange(count, dtype=jnp.float32)
    frame = 2.0 * CH
    shifted = (index + 0.5) / frame - TAPS / 2.0
    window = 0.5 - 0.5 * jnp.cos(2.0 * math.pi * (index + 0.5) / count)
    return (jnp.sinc(shifted) * window).astype(jnp.float32).reshape(TAPS, 2 * CH)

def twiddle():
    frame = 2 * CH
    chan = jnp.arange(CH, dtype=jnp.int32)[:, None]
    point = jnp.arange(frame, dtype=jnp.int32)[None, :]
    phase = (chan * point % frame).astype(jnp.float32) * (2.0 * math.pi / frame)
    table = jnp.stack([jnp.cos(phase), -jnp.sin(phase)], axis=1)
    return table.reshape(2 * CH, frame).astype(jnp.bfloat16)

def normalize(spectra, good):
    squares = lax.optimization_barrier(jnp.sum(spectra * spectra, axis=2))
    rows = squares.shape[1]
    power = lax.optimization_barrier(jnp.sum(squares.reshape(spectra.shape[0] // 2, 2, rows), axis=1)) / SPEC
    scale = good[None, :] / jnp.sqrt(power + 1e-05)
    return (spectra * jnp.repeat(scale, 2, axis=0)[:, :, None]).astype(jnp.bfloat16)

def channelize(group, good):
    taps = prototype()
    table = twiddle()
    frames = group.reshape(group.shape[0], SPEC + TAPS - 1, 2 * CH).astype(jnp.float32)
    total = jnp.zeros((group.shape[0], SPEC, 2 * CH), jnp.float32)
    for tap in range(TAPS):
        total = total + taps[tap][None, None, :] * frames[:, tap:tap + SPEC, :]
    fir = total.astype(jnp.bfloat16)
    spectra = jnp.einsum('kn,isn->kis', table.astype(jnp.float32), fir.astype(jnp.float32), precision=lax.Precision.HIGHEST)
    return normalize(spectra, good)

def correlate(pair):
    stacked = pair.reshape(2 * NIN, SPEC)
    gram = jnp.dot(stacked, stacked.T, preferred_element_type=jnp.float32)
    real_real = gram[:NIN, :NIN]
    real_imag = gram[:NIN, NIN:]
    imag_real = gram[NIN:, :NIN]
    imag_imag = gram[NIN:, NIN:]
    return jnp.stack([(real_real + imag_imag) / SPEC, (imag_real - real_imag) / SPEC], axis=0)

def reference(samples, slot_order, flags):
    group_size = math.gcd(NIN, 128)
    groups = NIN // group_size
    good = (1 - flags).astype(jnp.float32)
    quant = lax.map(lambda pair: channelize(pair[0], pair[1]), (samples.reshape(groups, group_size, NSAMP), good.reshape(groups, group_size)))
    quant = jnp.transpose(quant, (1, 0, 2, 3)).reshape(2 * CH, NIN, SPEC)
    quant = quant.reshape(CH, 2, NBLOCKS, BLOCK, SPEC)
    block_index = jnp.arange(NBLOCKS, dtype=jnp.int32)[:, None]
    slots = quant[:, :, block_index, slot_order, :].reshape(CH, 2, NIN, SPEC)
    return lax.map(correlate, slots)
```

```python
import functools
import math

import jax
import jax.numpy as jnp
from jax import lax
from jax.experimental import pallas as pl
from jax.experimental.pallas import tpu as pltpu
from jax.sharding import PartitionSpec as P

CH = 256
TAPS = 12
SPEC = 512
MESH = pl.DeviceIdType.MESH


def prototype():
    count = TAPS * 2 * CH
    index = jnp.arange(count, dtype=jnp.float32)
    frame = 2.0 * CH
    shifted = (index + 0.5) / frame - TAPS / 2.0
    window = 0.5 - 0.5 * jnp.cos(2.0 * math.pi * (index + 0.5) / count)
    return (jnp.sinc(shifted) * window).astype(jnp.float32).reshape(TAPS, 2 * CH)


def twiddle():
    frame = 2 * CH
    chan = jnp.arange(CH, dtype=jnp.int32)[:, None]
    point = jnp.arange(frame, dtype=jnp.int32)[None, :]
    phase = (chan * point % frame).astype(jnp.float32) * (2.0 * math.pi / frame)
    table = jnp.stack([jnp.cos(phase), -jnp.sin(phase)], axis=1)
    return table.reshape(2 * CH, frame).astype(jnp.bfloat16)


def tile(rows, cols):
    half = rows.shape[0] // 2
    gram = lax.dot_general(rows, cols, (((1,), (1,)), ((), ())), preferred_element_type=jnp.float32)
    real = gram[:half, :half] + gram[half:, half:]
    imag = gram[half:, :half] - gram[:half, half:]
    return real * (1.0 / SPEC), imag * (1.0 / SPEC)


def correlate_kernel(n, own, out, rbuf, lbuf, tls, tlr, trs, trr,
                     rsend, rrecv, lsend, lrecv, tlsend, tlrecv, trsend, trrecv):
    me = lax.axis_index("blk")
    depth, chans, block = n // 2, own.shape[0], own.shape[1] // 2
    dr = depth - lax.rem(lax.axis_index("freq"), 2)
    dl = n - 1 - dr

    def right(t, c, src):
        return pltpu.make_async_remote_copy(
            src, rbuf.at[t, c], rsend.at[t, c], rrecv.at[t, c],
            device_id={"blk": lax.rem(me + 1, n)}, device_id_type=MESH)

    def left(t, c, src):
        return pltpu.make_async_remote_copy(
            src, lbuf.at[t, c], lsend.at[t, c], lrecv.at[t, c],
            device_id={"blk": lax.rem(me + n - 1, n)}, device_id_type=MESH)

    def tile_left(k, c):
        return pltpu.make_async_remote_copy(
            tls.at[k - 1, c], tlr.at[k - 1, c], tlsend.at[k - 1, c], tlrecv.at[k - 1, c],
            device_id={"blk": lax.rem(me + n - k, n)}, device_id_type=MESH)

    def tile_right(k, c):
        return pltpu.make_async_remote_copy(
            trs.at[k - 1, c], trr.at[k - 1, c], trsend.at[k - 1, c], trrecv.at[k - 1, c],
            device_id={"blk": lax.rem(me + k, n)}, device_id_type=MESH)

    def put(c, column, real, imag):
        at = pl.ds(pl.multiple_of(column * block, block), block)
        out[c, 0, :, at] = real.astype(jnp.float32)
        out[c, 1, :, at] = imag.astype(jnp.float32)

    barrier = pltpu.get_barrier_semaphore()
    for k in range(1, n):
        pl.semaphore_signal(barrier, 1, device_id={"blk": lax.rem(me + k, n)}, device_id_type=MESH)
    pl.semaphore_wait(barrier, n - 1)

    for c in range(chans):
        @pl.when(me < n - 1)
        def _():
            right(0, c, own.at[c]).start()

        @pl.when(me > 0)
        def _():
            left(0, c, own.at[c]).start()

    @pl.loop(0, chans)
    def _(c):
        put(c, me, *tile(own[c], own[c]))

    @pl.loop(0, depth)
    def _(t):
        from_left = (t < dr) & (me - 1 - t >= 0)
        from_right = (t < dl) & (me + 1 + t < n)

        @pl.loop(0, chans)
        def _(c):
            @pl.when(from_left)
            def _():
                right(t, c, own.at[c]).wait_recv()

                @pl.when((t + 1 < dr) & (me < n - 1))
                def _():
                    right(t + 1, c, rbuf.at[t, c]).start()

            @pl.when(from_right)
            def _():
                left(t, c, own.at[c]).wait_recv()

                @pl.when((t + 1 < dl) & (me > 0))
                def _():
                    left(t + 1, c, lbuf.at[t, c]).start()

            @pl.loop(1, depth + 1)
            def _(k):
                @pl.when((me + dl < n) & (me - k >= 0) & (k <= dr) & (jnp.maximum(k, dl) == t + 1))
                def _():
                    real, imag = tile(rbuf[k - 1, c], lbuf[dl - 1, c])
                    tls[k - 1, c, 0] = real.astype(jnp.bfloat16)
                    tls[k - 1, c, 1] = imag.astype(jnp.bfloat16)
                    tile_left(k, c).start()

                @pl.when((me - dr >= 0) & (me + k < n) & (k <= dl) & (jnp.maximum(k, dr) == t + 1))
                def _():
                    real, imag = tile(lbuf[k - 1, c], rbuf[dr - 1, c])
                    trs[k - 1, c, 0] = real.astype(jnp.bfloat16)
                    trs[k - 1, c, 1] = imag.astype(jnp.bfloat16)
                    tile_right(k, c).start()

            @pl.when(from_left)
            def _():
                put(c, me - 1 - t, *tile(own[c], rbuf[t, c]))

            @pl.when(from_right)
            def _():
                put(c, me + 1 + t, *tile(own[c], lbuf[t, c]))

    @pl.loop(0, chans)
    def _(c):
        @pl.loop(1, depth + 1)
        def _(k):
            @pl.when((me + k + dl < n) & (k <= dr))
            def _():
                tile_left(k, c).wait_recv()
                put(c, me + k + dl, tlr[k - 1, c, 0], tlr[k - 1, c, 1])

            @pl.when((me - k - dr >= 0) & (k <= dl))
            def _():
                tile_right(k, c).wait_recv()
                put(c, me - k - dr, trr[k - 1, c, 0], trr[k - 1, c, 1])

    @pl.loop(0, chans)
    def _(c):
        @pl.loop(0, depth)
        def _(t):
            @pl.when((t < dr) & (me - t >= 0) & (me < n - 1))
            def _():
                right(t, c, own.at[c]).wait_send()

            @pl.when((t < dl) & (me + t < n) & (me > 0))
            def _():
                left(t, c, own.at[c]).wait_send()

            @pl.when((me + dl < n) & (me - t - 1 >= 0) & (t + 1 <= dr))
            def _():
                tile_left(t + 1, c).wait_send()

            @pl.when((me - dr >= 0) & (me + t + 1 < n) & (t + 1 <= dl))
            def _():
                tile_right(t + 1, c).wait_send()


def correlate(n, own):
    chans, rows, spec = own.shape
    depth, block = n // 2, rows // 2
    held = pltpu.VMEM((depth, chans, rows, spec), jnp.bfloat16)
    tiles = pltpu.VMEM((depth, chans, 2, block, block), jnp.bfloat16)
    sems = pltpu.SemaphoreType.DMA((depth, chans))
    return pl.pallas_call(
        functools.partial(correlate_kernel, n),
        out_shape=jax.ShapeDtypeStruct((chans, 2, block, n * block), jnp.float32),
        in_specs=[pl.BlockSpec(memory_space=pltpu.VMEM)],
        out_specs=pl.BlockSpec(memory_space=pltpu.VMEM),
        scratch_shapes=[held, held, tiles, tiles, tiles, tiles] + [sems] * 8,
        compiler_params=pltpu.CompilerParams(
            collective_id=0, has_side_effects=True, vmem_limit_bytes=48 << 20),
    )(own)


def body(n, samples, slot_order, flags):
    inputs = samples.shape[0]
    taps = prototype()
    table = twiddle()
    good = (1 - flags).astype(jnp.float32)
    frames = samples.reshape(inputs, SPEC + TAPS - 1, 2 * CH)
    total = jnp.zeros((inputs, SPEC, 2 * CH), jnp.float32)
    for tap in range(TAPS):
        total = total + taps[tap][None, None, :] * frames[:, tap : tap + SPEC, :].astype(jnp.float32)
    fir = total.astype(jnp.bfloat16)
    spectra = jnp.einsum("kn,isn->iks", table, fir, preferred_element_type=jnp.float32)
    squares = jnp.sum(spectra * spectra, axis=2)
    power = jnp.sum(squares.reshape(inputs, CH, 2), axis=2) / SPEC
    scale = good[:, None] / jnp.sqrt(power + 1e-05)
    quantized = (spectra * jnp.repeat(scale, 2, axis=1)[:, :, None]).astype(jnp.bfloat16)

    groups = lax.axis_size("freq")
    rows = 2 * CH // groups
    leaving = quantized.reshape(inputs, groups, rows, SPEC).transpose(1, 0, 2, 3)
    arrived = lax.all_to_all(leaving.reshape(groups, inputs * rows, SPEC), "freq", 0, 0, tiled=True)
    block = groups * inputs
    arranged = jnp.take(arrived.reshape(block, rows, SPEC), slot_order[0], axis=0)
    own = arranged.transpose(1, 0, 2).reshape(rows // 2, 2 * block, SPEC)
    return correlate(n, own)


def solution(mesh):
    in_specs = (P(("blk", "freq"), None), P("blk", None), P(("blk", "freq")))
    out_specs = P("freq", None, "blk", None)
    return jax.shard_map(
        functools.partial(body, mesh.shape["blk"]), mesh=mesh, in_specs=in_specs, out_specs=out_specs, check_vma=False)
```

```python
import functools
import math

import jax
import jax.numpy as jnp
from jax import lax
from jax.experimental import pallas as pl
from jax.experimental.pallas import tpu as pltpu
from jax.sharding import PartitionSpec as P

CH = 256
TAPS = 12
SPEC = 512
MESH = pl.DeviceIdType.MESH


def prototype():
    count = TAPS * 2 * CH
    index = jnp.arange(count, dtype=jnp.float32)
    frame = 2.0 * CH
    shifted = (index + 0.5) / frame - TAPS / 2.0
    window = 0.5 - 0.5 * jnp.cos(2.0 * math.pi * (index + 0.5) / count)
    return (jnp.sinc(shifted) * window).astype(jnp.float32).reshape(TAPS, 2 * CH)


def twiddle():
    frame = 2 * CH
    chan = jnp.arange(CH, dtype=jnp.int32)[:, None]
    point = jnp.arange(frame, dtype=jnp.int32)[None, :]
    phase = (chan * point % frame).astype(jnp.float32) * (2.0 * math.pi / frame)
    table = jnp.stack([jnp.cos(phase), -jnp.sin(phase)], axis=1)
    return table.reshape(2 * CH, frame).astype(jnp.bfloat16)


def tile(rows, cols):
    half = rows.shape[0] // 2
    gram = lax.dot_general(rows, cols, (((1,), (1,)), ((), ())), preferred_element_type=jnp.float32)
    real = gram[:half, :half] + gram[half:, half:]
    imag = gram[half:, :half] - gram[:half, half:]
    return real * (1.0 / SPEC), imag * (1.0 / SPEC)


def correlate_kernel(n, own, out, nbuf, fbuf, ts, tr, nsend, nrecv, frecv, tsend, trecv):
    me = lax.axis_index("blk")
    half, chans, block = n // 2, own.shape[0], own.shape[1] // 2
    mid = half - 1
    side = me // half
    step = 1 - 2 * side
    place = me * step + (n - 1) * side
    inner = {"blk": me + step}

    def pass_near(t, c, src):
        return pltpu.make_async_remote_copy(
            src, nbuf.at[t, c], nsend.at[t, c], nrecv.at[t, c], device_id=inner, device_id_type=MESH)

    def pass_far(t, c, src):
        return pltpu.make_async_remote_copy(
            src, fbuf.at[t, c], nsend.at[t, c], frecv.at[t, c], device_id=inner, device_id_type=MESH)

    def give(t, v, slot, c):
        return pltpu.make_async_remote_copy(
            ts.at[t, v, c], tr.at[slot, c], tsend.at[t, v, c], trecv.at[slot, c],
            device_id={"blk": lax.rem(me - (t + 1) * step + n, n)}, device_id_type=MESH)

    def start(t, c, src):
        @pl.when(place < mid)
        def _():
            pass_near(t, c, src).start()

        @pl.when(place == mid)
        def _():
            pass_far(t, c, src).start()

    def put(c, column, real, imag):
        at = pl.ds(pl.multiple_of(column * block, block), block)
        out[c, 0, :, at] = real.astype(jnp.float32)
        out[c, 1, :, at] = imag.astype(jnp.float32)

    def relay(t, v, slot, c, rows, cols):
        real, imag = tile(rows, cols)
        ts[t, v, c, 0] = real.astype(jnp.bfloat16)
        ts[t, v, c, 1] = imag.astype(jnp.bfloat16)
        give(t, v, slot, c).start()

    barrier = pltpu.get_barrier_semaphore()
    for k in range(1, n):
        pl.semaphore_signal(barrier, 1, device_id={"blk": lax.rem(me + k, n)}, device_id_type=MESH)
    pl.semaphore_wait(barrier, n - 1)

    for c in range(chans):
        start(0, c, own.at[c])

    @pl.loop(0, chans)
    def _(c):
        put(c, me, *tile(own[c], own[c]))

    @pl.loop(0, half)
    def _(t):
        @pl.loop(0, chans)
        def _(c):
            @pl.when(t < place)
            def _():
                pass_near(t, c, own.at[c]).wait_recv()
                start(t + 1, c, nbuf.at[t, c])

            @pl.when(place == mid)
            def _():
                pass_far(t, c, own.at[c]).wait_recv()

            @pl.when(t < place)
            def _():
                relay(t, 0, place, c, nbuf[t, c], own[c])

            @pl.when(place == mid)
            def _():
                @pl.loop(0, mid)
                def _(r):
                    @pl.when(r <= t)
                    def _():
                        relay(r, 1 + t, half + t, c, nbuf[r, c], fbuf[t, c])

                @pl.when(t < mid)
                def _():
                    @pl.loop(0, mid)
                    def _(u):
                        @pl.when(u < t)
                        def _():
                            relay(t, 1 + u, half + u, c, nbuf[t, c], fbuf[u, c])

                put(c, me + (t + 1) * step, *tile(own[c], fbuf[t, c]))

            @pl.when(t < place)
            def _():
                put(c, me - (t + 1) * step, *tile(own[c], nbuf[t, c]))

    @pl.when(place < mid)
    def _():
        @pl.loop(0, n)
        def _(slot):
            @pl.when(slot > place)
            def _():
                @pl.loop(0, chans)
                def _(c):
                    give(0, 0, slot, c).wait_recv()
                    put(c, me + (slot - place) * step, tr[slot, c, 0], tr[slot, c, 1])

    @pl.loop(0, chans)
    def _(c):
        @pl.loop(0, half)
        def _(t):
            @pl.when(t <= place)
            def _():
                pass_far(t, c, own.at[c]).wait_send()

            @pl.when(t < place)
            def _():
                give(t, 0, 0, c).wait_send()

            @pl.when((place == mid) & (t < mid))
            def _():
                @pl.loop(1, half + 1)
                def _(v):
                    give(t, v, 0, c).wait_send()


def correlate(n, own):
    chans, rows, spec = own.shape
    half, block = n // 2, rows // 2
    near = pltpu.VMEM((half - 1, chans, rows, spec), jnp.bfloat16)
    far = pltpu.VMEM((half, chans, rows, spec), jnp.bfloat16)
    leaving = pltpu.VMEM((half - 1, half + 1, chans, 2, block, block), jnp.bfloat16)
    arriving = pltpu.VMEM((n, chans, 2, block, block), jnp.bfloat16)
    dma = pltpu.SemaphoreType.DMA
    return pl.pallas_call(
        functools.partial(correlate_kernel, n),
        out_shape=jax.ShapeDtypeStruct((chans, 2, block, n * block), jnp.float32),
        in_specs=[pl.BlockSpec(memory_space=pltpu.VMEM)],
        out_specs=pl.BlockSpec(memory_space=pltpu.VMEM),
        scratch_shapes=[
            near, far, leaving, arriving, dma((half, chans)), dma((half - 1, chans)), dma((half, chans)),
            dma((half - 1, half + 1, chans)), dma((n, chans))],
        compiler_params=pltpu.CompilerParams(
            collective_id=0, has_side_effects=True, vmem_limit_bytes=48 << 20),
    )(own)


def body(n, samples, slot_order, flags):
    inputs = samples.shape[0]
    taps = prototype()
    table = twiddle()
    good = (1 - flags).astype(jnp.float32)
    frames = samples.reshape(inputs, SPEC + TAPS - 1, 2 * CH)
    total = jnp.zeros((inputs, SPEC, 2 * CH), jnp.float32)
    for tap in range(TAPS):
        total = total + taps[tap][None, None, :] * frames[:, tap : tap + SPEC, :].astype(jnp.float32)
    fir = total.astype(jnp.bfloat16)
    spectra = jnp.einsum("kn,isn->iks", table, fir, preferred_element_type=jnp.float32)
    squares = jnp.sum(spectra * spectra, axis=2)
    power = jnp.sum(squares.reshape(inputs, CH, 2), axis=2) / SPEC
    scale = good[:, None] / jnp.sqrt(power + 1e-05)
    quantized = (spectra * jnp.repeat(scale, 2, axis=1)[:, :, None]).astype(jnp.bfloat16)

    groups = lax.axis_size("freq")
    rows = 2 * CH // groups
    leaving = quantized.reshape(inputs, groups, rows, SPEC).transpose(1, 0, 2, 3)
    arrived = lax.all_to_all(leaving.reshape(groups, inputs * rows, SPEC), "freq", 0, 0, tiled=True)
    block = groups * inputs
    arranged = jnp.take(arrived.reshape(block, rows, SPEC), slot_order[0], axis=0)
    own = arranged.transpose(1, 0, 2).reshape(rows // 2, 2 * block, SPEC)
    return correlate(n, own)


def solution(mesh):
    in_specs = (P(("blk", "freq"), None), P("blk", None), P(("blk", "freq")))
    out_specs = P("freq", None, "blk", None)
    return jax.shard_map(
        functools.partial(body, mesh.shape["blk"]), mesh=mesh, in_specs=in_specs, out_specs=out_specs, check_vma=False)
```

```python
import functools
import math

import jax
import jax.numpy as jnp
from jax import lax
from jax.experimental import pallas as pl
from jax.experimental.pallas import tpu as pltpu
from jax.sharding import PartitionSpec as P

CH = 256
TAPS = 12
SPEC = 512
MESH = pl.DeviceIdType.MESH


def prototype():
    count = TAPS * 2 * CH
    index = jnp.arange(count, dtype=jnp.float32)
    frame = 2.0 * CH
    shifted = (index + 0.5) / frame - TAPS / 2.0
    window = 0.5 - 0.5 * jnp.cos(2.0 * math.pi * (index + 0.5) / count)
    return (jnp.sinc(shifted) * window).astype(jnp.float32).reshape(TAPS, 2 * CH)


def twiddle():
    frame = 2 * CH
    chan = jnp.arange(CH, dtype=jnp.int32)[:, None]
    point = jnp.arange(frame, dtype=jnp.int32)[None, :]
    phase = (chan * point % frame).astype(jnp.float32) * (2.0 * math.pi / frame)
    table = jnp.stack([jnp.cos(phase), -jnp.sin(phase)], axis=1)
    return table.reshape(2 * CH, frame).astype(jnp.bfloat16)


def tile(rows, cols):
    half = rows.shape[0] // 2
    gram = lax.dot_general(rows, cols, (((1,), (1,)), ((), ())), preferred_element_type=jnp.float32)
    real = gram[:half, :half] + gram[half:, half:]
    imag = gram[half:, :half] - gram[:half, half:]
    return real * (1.0 / SPEC), imag * (1.0 / SPEC)


def correlate_kernel(n, keep, swap, place_keep, place_swap, out, own, xbuf, xsend, xrecv, nbuf, fbuf, ts, tr, nsend, nrecv, frecv, tsend, trecv):
    me = lax.axis_index("blk")
    half, chans, block = n // 2, own.shape[0], own.shape[1] // 2
    mid = half - 1
    side = me // half
    step = 1 - 2 * side
    place = me * step + (n - 1) * side
    inner = {"blk": me + step}

    def pass_near(t, c, src):
        return pltpu.make_async_remote_copy(
            src, nbuf.at[t, c], nsend.at[t, c], nrecv.at[t, c], device_id=inner, device_id_type=MESH)

    def pass_far(t, c, src):
        return pltpu.make_async_remote_copy(
            src, fbuf.at[t, c], nsend.at[t, c], frecv.at[t, c], device_id=inner, device_id_type=MESH)

    def give(t, v, slot, c):
        return pltpu.make_async_remote_copy(
            ts.at[t, v, c], tr.at[slot, c], tsend.at[t, v, c], trecv.at[slot, c],
            device_id={"blk": lax.rem(me - (t + 1) * step + n, n)}, device_id_type=MESH)

    def start(t, c, src):
        @pl.when(place < mid)
        def _():
            pass_near(t, c, src).start()

        @pl.when(place == mid)
        def _():
            pass_far(t, c, src).start()

    def put(c, column, real, imag):
        at = pl.ds(pl.multiple_of(column * block, block), block)
        out[c, 0, :, at] = real.astype(jnp.float32)
        out[c, 1, :, at] = imag.astype(jnp.float32)

    def relay(t, v, slot, c, rows, cols):
        real, imag = tile(rows, cols)
        ts[t, v, c, 0] = real.astype(jnp.bfloat16)
        ts[t, v, c, 1] = imag.astype(jnp.bfloat16)
        give(t, v, slot, c).start()

    group = lax.axis_index("freq")
    partner = {"freq": group + 2 - 4 * lax.rem(group // 2, 2)}

    def exchange(c):
        return pltpu.make_async_remote_copy(
            swap.at[c], xbuf.at[c], xsend.at[c], xrecv.at[c], device_id=partner, device_id_type=MESH)

    barrier = pltpu.get_barrier_semaphore()
    for k in range(1, n):
        pl.semaphore_signal(barrier, 1, device_id={"blk": lax.rem(me + k, n)}, device_id_type=MESH)
    pl.semaphore_signal(barrier, 1, device_id=partner, device_id_type=MESH)
    pl.semaphore_wait(barrier, n)

    for c in range(chans):
        exchange(c).start()

    @pl.loop(0, chans)
    def _(c):
        exchange(c).wait_recv()
        for p in range(2):
            rows = pl.ds(p * (block // 2), block // 2)
            mixed = jnp.dot(place_keep[...], keep[c, rows, :], preferred_element_type=jnp.float32)
            mixed += jnp.dot(place_swap[...], xbuf[c, rows, :], preferred_element_type=jnp.float32)
            own[c, pl.ds(p * block, block), :] = mixed.astype(jnp.bfloat16)
        start(0, c, own.at[c])

    @pl.loop(0, chans)
    def _(c):
        exchange(c).wait_send()
        put(c, me, *tile(own[c], own[c]))

    @pl.loop(0, half)
    def _(t):
        @pl.loop(0, chans)
        def _(c):
            @pl.when(t < place)
            def _():
                pass_near(t, c, own.at[c]).wait_recv()
                start(t + 1, c, nbuf.at[t, c])

            @pl.when(place == mid)
            def _():
                pass_far(t, c, own.at[c]).wait_recv()

            @pl.when(t < place)
            def _():
                relay(t, 0, place, c, nbuf[t, c], own[c])

            @pl.when(place == mid)
            def _():
                @pl.loop(0, mid)
                def _(r):
                    @pl.when(r <= t)
                    def _():
                        relay(r, 1 + t, half + t, c, nbuf[r, c], fbuf[t, c])

                @pl.when(t < mid)
                def _():
                    @pl.loop(0, mid)
                    def _(u):
                        @pl.when(u < t)
                        def _():
                            relay(t, 1 + u, half + u, c, nbuf[t, c], fbuf[u, c])

                put(c, me + (t + 1) * step, *tile(own[c], fbuf[t, c]))

            @pl.when(t < place)
            def _():
                put(c, me - (t + 1) * step, *tile(own[c], nbuf[t, c]))

    @pl.when(place < mid)
    def _():
        @pl.loop(0, n)
        def _(slot):
            @pl.when(slot > place)
            def _():
                @pl.loop(0, chans)
                def _(c):
                    give(0, 0, slot, c).wait_recv()
                    put(c, me + (slot - place) * step, tr[slot, c, 0], tr[slot, c, 1])

    @pl.loop(0, chans)
    def _(c):
        @pl.loop(0, half)
        def _(t):
            @pl.when(t <= place)
            def _():
                pass_far(t, c, own.at[c]).wait_send()

            @pl.when(t < place)
            def _():
                give(t, 0, 0, c).wait_send()

            @pl.when((place == mid) & (t < mid))
            def _():
                @pl.loop(1, half + 1)
                def _(v):
                    give(t, v, 0, c).wait_send()


def correlate(n, keep, swap, place_keep, place_swap):
    chans, block, spec = keep.shape
    half, rows = n // 2, 2 * block
    own = pltpu.VMEM((chans, rows, spec), jnp.bfloat16)
    near = pltpu.VMEM((half - 1, chans, rows, spec), jnp.bfloat16)
    far = pltpu.VMEM((half, chans, rows, spec), jnp.bfloat16)
    leaving = pltpu.VMEM((half - 1, half + 1, chans, 2, block, block), jnp.bfloat16)
    arriving = pltpu.VMEM((n, chans, 2, block, block), jnp.bfloat16)
    dma = pltpu.SemaphoreType.DMA
    return pl.pallas_call(
        functools.partial(correlate_kernel, n),
        out_shape=jax.ShapeDtypeStruct((chans, 2, block, n * block), jnp.float32),
        in_specs=[pl.BlockSpec(memory_space=pltpu.VMEM)] * 4,
        out_specs=pl.BlockSpec(memory_space=pltpu.VMEM),
        scratch_shapes=[
            own, pltpu.VMEM(keep.shape, jnp.bfloat16), dma((chans,)), dma((chans,)),
            near, far, leaving, arriving, dma((half, chans)), dma((half - 1, chans)), dma((half, chans)),
            dma((half - 1, half + 1, chans)), dma((n, chans))],
        compiler_params=pltpu.CompilerParams(
            collective_id=0, has_side_effects=True, vmem_limit_bytes=48 << 20),
    )(keep, swap, place_keep, place_swap)


def body(n, samples, slot_order, flags):
    inputs = samples.shape[0]
    taps = prototype()
    table = twiddle()
    good = (1 - flags).astype(jnp.float32)
    frames = samples.reshape(inputs, SPEC + TAPS - 1, 2 * CH)
    total = jnp.zeros((inputs, SPEC, 2 * CH), jnp.float32)
    for tap in range(TAPS):
        total = total + taps[tap][None, None, :] * frames[:, tap : tap + SPEC, :].astype(jnp.float32)
    fir = total.astype(jnp.bfloat16)
    spectra = jnp.einsum("kn,isn->iks", table, fir, preferred_element_type=jnp.float32)
    squares = jnp.sum(spectra * spectra, axis=2)
    power = jnp.sum(squares.reshape(inputs, CH, 2), axis=2) / SPEC
    scale = good[:, None] / jnp.sqrt(power + 1e-05)
    quantized = (spectra * jnp.repeat(scale, 2, axis=1)[:, :, None]).astype(jnp.bfloat16)

    groups = lax.axis_size("freq")
    rows, columns = 2 * CH // groups, groups // 4
    plane = [[f for f in range(groups) if f // 2 % 2 == z] for z in range(2)]
    leaving = quantized.reshape(inputs, columns, 2, 2, rows, SPEC).transpose(1, 3, 2, 0, 4, 5)
    arrived = lax.all_to_all(
        leaving.reshape(2 * columns, 2 * inputs * rows, SPEC), "freq", 0, 0, axis_index_groups=plane, tiled=True)
    held = 2 * columns * inputs
    halves = arrived.reshape(2 * columns, 2, inputs, rows, SPEC).transpose(1, 3, 0, 2, 4)
    halves = halves.reshape(2, rows // 2, 2 * held, SPEC)
    z = lax.axis_index("freq") // 2 % 2
    keep = lax.dynamic_index_in_dim(halves, z, 0, keepdims=False)
    swap = lax.dynamic_index_in_dim(halves, 1 - z, 0, keepdims=False)
    wanted = slot_order[0]
    chip = 2 * inputs
    inside = wanted // (2 * chip) * chip + wanted % chip
    onehot = inside[:, None] == jnp.arange(held)[None, :]
    here = (wanted // chip % 2 == z)[:, None]
    return correlate(
        n, keep, swap, (onehot & here).astype(jnp.bfloat16), (onehot & ~here).astype(jnp.bfloat16))


def solution(mesh):
    in_specs = (P(("blk", "freq"), None), P("blk", None), P(("blk", "freq")))
    out_specs = P("freq", None, "blk", None)
    return jax.shard_map(
        functools.partial(body, mesh.shape["blk"]), mesh=mesh, in_specs=in_specs, out_specs=out_specs, check_vma=False)
```

```python
import functools
import math

import jax
import jax.numpy as jnp
import ml_dtypes
import numpy as np
from jax import lax
from jax.experimental import pallas as pl
from jax.experimental.pallas import tpu as pltpu
from jax.sharding import PartitionSpec as P

CH = 256
TAPS = 12
SPEC = 512
MESH = pl.DeviceIdType.MESH


def prototype():
    count = TAPS * 2 * CH
    index = jnp.arange(count, dtype=jnp.float32)
    frame = 2.0 * CH
    shifted = (index + 0.5) / frame - TAPS / 2.0
    window = 0.5 - 0.5 * jnp.cos(2.0 * math.pi * (index + 0.5) / count)
    return (jnp.sinc(shifted) * window).astype(jnp.float32).reshape(TAPS, 2 * CH)


def twiddle():
    frame = 2 * CH
    phase = np.arange(CH)[:, None] * np.arange(frame)[None, :] % frame * (2.0 * math.pi / frame)
    table = np.stack([np.cos(phase), -np.sin(phase)], axis=1)
    return table.reshape(2 * CH, frame).astype(np.float32).astype(ml_dtypes.bfloat16)


def tile(rows, cols):
    half = rows.shape[0] // 2
    gram = lax.dot_general(rows, cols, (((1,), (1,)), ((), ())), preferred_element_type=jnp.float32)
    real = gram[:half, :half] + gram[half:, half:]
    imag = gram[half:, :half] - gram[:half, half:]
    return real * (1.0 / SPEC), imag * (1.0 / SPEC)


def correlate_kernel(n, halves, place_keep, place_swap, out, own, xbuf, xsend, xrecv, nbuf, fbuf, ts, tr, nsend, nrecv, frecv, tsend, trecv):
    me = lax.axis_index("blk")
    half, chans, block = n // 2, own.shape[0], own.shape[1] // 2
    mid = half - 1
    side = me // half
    step = 1 - 2 * side
    place = me * step + (n - 1) * side
    inner = {"blk": me + step}

    def pass_near(t, c, src):
        return pltpu.make_async_remote_copy(
            src, nbuf.at[t, c], nsend.at[t, c], nrecv.at[t, c], device_id=inner, device_id_type=MESH)

    def pass_far(t, c, src):
        return pltpu.make_async_remote_copy(
            src, fbuf.at[t, c], nsend.at[t, c], frecv.at[t, c], device_id=inner, device_id_type=MESH)

    def give(t, v, slot, c):
        return pltpu.make_async_remote_copy(
            ts.at[t, v, c], tr.at[slot, c], tsend.at[t, v, c], trecv.at[slot, c],
            device_id={"blk": lax.rem(me - (t + 1) * step + n, n)}, device_id_type=MESH)

    def start(t, c, src):
        @pl.when(place < mid)
        def _():
            pass_near(t, c, src).start()

        @pl.when(place == mid)
        def _():
            pass_far(t, c, src).start()

    def put(c, column, real, imag):
        at = pl.ds(pl.multiple_of(column * block, block), block)
        out[c, 0, :, at] = real.astype(jnp.float32)
        out[c, 1, :, at] = imag.astype(jnp.float32)

    def relay(t, v, slot, c, rows, cols):
        real, imag = tile(rows, cols)
        ts[t, v, c, 0] = real.astype(jnp.bfloat16)
        ts[t, v, c, 1] = imag.astype(jnp.bfloat16)
        give(t, v, slot, c).start()

    group = lax.axis_index("freq")
    z = lax.rem(group // 2, 2)
    partner = {"freq": group + 2 - 4 * z}

    def exchange(c):
        return pltpu.make_async_remote_copy(
            halves.at[1 - z, c], xbuf.at[c], xsend.at[c], xrecv.at[c], device_id=partner, device_id_type=MESH)

    barrier = pltpu.get_barrier_semaphore()
    for k in range(1, n):
        pl.semaphore_signal(barrier, 1, device_id={"blk": lax.rem(me + k, n)}, device_id_type=MESH)
    pl.semaphore_signal(barrier, 1, device_id=partner, device_id_type=MESH)
    pl.semaphore_wait(barrier, n)

    for c in range(chans):
        exchange(c).start()

    @pl.loop(0, chans)
    def _(c):
        exchange(c).wait_recv()
        for p in range(2):
            rows = pl.ds(p * (block // 2), block // 2)
            mixed = jnp.dot(place_keep[...], halves[z, c, rows, :], preferred_element_type=jnp.float32)
            mixed += jnp.dot(place_swap[...], xbuf[c, rows, :], preferred_element_type=jnp.float32)
            own[c, pl.ds(p * block, block), :] = mixed.astype(jnp.bfloat16)
        start(0, c, own.at[c])

    @pl.loop(0, chans)
    def _(c):
        exchange(c).wait_send()
        put(c, me, *tile(own[c], own[c]))

    @pl.loop(0, half)
    def _(t):
        @pl.loop(0, chans)
        def _(c):
            @pl.when(t < place)
            def _():
                pass_near(t, c, own.at[c]).wait_recv()
                start(t + 1, c, nbuf.at[t, c])

            @pl.when(place == mid)
            def _():
                pass_far(t, c, own.at[c]).wait_recv()

            @pl.when(t < place)
            def _():
                relay(t, 0, place, c, nbuf[t, c], own[c])

            @pl.when(place == mid)
            def _():
                @pl.loop(0, mid)
                def _(k):
                    r = mid - 1 - k

                    @pl.when(r <= t)
                    def _():
                        relay(r, 1 + t, half + t, c, nbuf[r, c], fbuf[t, c])

                @pl.when(t < mid)
                def _():
                    @pl.loop(0, mid)
                    def _(u):
                        @pl.when(u < t)
                        def _():
                            relay(t, 1 + u, half + u, c, nbuf[t, c], fbuf[u, c])

                put(c, me + (t + 1) * step, *tile(own[c], fbuf[t, c]))

            @pl.when(t < place)
            def _():
                put(c, me - (t + 1) * step, *tile(own[c], nbuf[t, c]))

    @pl.when(place < mid)
    def _():
        @pl.loop(0, n)
        def _(slot):
            @pl.when(slot > place)
            def _():
                @pl.loop(0, chans)
                def _(c):
                    give(0, 0, slot, c).wait_recv()
                    put(c, me + (slot - place) * step, tr[slot, c, 0], tr[slot, c, 1])

    @pl.loop(0, chans)
    def _(c):
        @pl.loop(0, half)
        def _(t):
            @pl.when(t <= place)
            def _():
                pass_far(t, c, own.at[c]).wait_send()

            @pl.when(t < place)
            def _():
                give(t, 0, 0, c).wait_send()

            @pl.when((place == mid) & (t < mid))
            def _():
                @pl.loop(1, half + 1)
                def _(v):
                    give(t, v, 0, c).wait_send()


def correlate(n, halves, place_keep, place_swap):
    _, chans, block, spec = halves.shape
    half, rows = n // 2, 2 * block
    own = pltpu.VMEM((chans, rows, spec), jnp.bfloat16)
    near = pltpu.VMEM((half - 1, chans, rows, spec), jnp.bfloat16)
    far = pltpu.VMEM((half, chans, rows, spec), jnp.bfloat16)
    leaving = pltpu.VMEM((half - 1, half + 1, chans, 2, block, block), jnp.bfloat16)
    arriving = pltpu.VMEM((n, chans, 2, block, block), jnp.bfloat16)
    dma = pltpu.SemaphoreType.DMA
    return pl.pallas_call(
        functools.partial(correlate_kernel, n),
        out_shape=jax.ShapeDtypeStruct((chans, 2, block, n * block), jnp.float32),
        in_specs=[pl.BlockSpec(memory_space=pltpu.VMEM)] * 3,
        out_specs=pl.BlockSpec(memory_space=pltpu.VMEM),
        scratch_shapes=[
            own, pltpu.VMEM(halves.shape[1:], jnp.bfloat16), dma((chans,)), dma((chans,)),
            near, far, leaving, arriving, dma((half, chans)), dma((half - 1, chans)), dma((half, chans)),
            dma((half - 1, half + 1, chans)), dma((n, chans))],
        compiler_params=pltpu.CompilerParams(
            collective_id=0, has_side_effects=True, vmem_limit_bytes=48 << 20),
    )(halves, place_keep, place_swap)


def body(n, samples, slot_order, flags):
    inputs = samples.shape[0]
    taps = prototype()
    table = jnp.asarray(twiddle())
    good = (1 - flags).astype(jnp.float32)
    frames = samples.reshape(inputs, SPEC + TAPS - 1, 2 * CH)
    total = jnp.zeros((inputs, SPEC, 2 * CH), jnp.float32)
    for tap in range(TAPS):
        total = total + taps[tap][None, None, :] * frames[:, tap : tap + SPEC, :].astype(jnp.float32)
    fir = total.astype(jnp.bfloat16)
    spectra = jnp.einsum("kn,isn->iks", table, fir, preferred_element_type=jnp.float32)
    squares = jnp.sum(spectra * spectra, axis=2)
    power = jnp.sum(squares.reshape(inputs, CH, 2), axis=2) / SPEC
    scale = good[:, None] / jnp.sqrt(power + 1e-05)
    quantized = (spectra * jnp.repeat(scale, 2, axis=1)[:, :, None]).astype(jnp.bfloat16)

    groups = lax.axis_size("freq")
    rows, columns = 2 * CH // groups, groups // 4
    plane = [[f for f in range(groups) if f // 2 % 2 == z] for z in range(2)]
    leaving = quantized.reshape(inputs, columns, 2, 2, rows, SPEC).transpose(1, 3, 2, 0, 4, 5)
    arrived = lax.all_to_all(
        leaving.reshape(2 * columns, 2 * inputs * rows, SPEC), "freq", 0, 0, axis_index_groups=plane, tiled=True)
    held = 2 * columns * inputs
    halves = arrived.reshape(2 * columns, 2, inputs, rows, SPEC).transpose(1, 3, 0, 2, 4)
    halves = halves.reshape(2, rows // 2, 2 * held, SPEC)
    z = lax.axis_index("freq") // 2 % 2
    wanted = slot_order[0]
    chip = 2 * inputs
    inside = wanted // (2 * chip) * chip + wanted % chip
    onehot = inside[:, None] == jnp.arange(held)[None, :]
    here = (wanted // chip % 2 == z)[:, None]
    return correlate(
        n, halves, (onehot & here).astype(jnp.bfloat16), (onehot & ~here).astype(jnp.bfloat16))


def solution(mesh):
    in_specs = (P(("blk", "freq"), None), P("blk", None), P(("blk", "freq")))
    out_specs = P("freq", None, "blk", None)
    return jax.shard_map(
        functools.partial(body, mesh.shape["blk"]), mesh=mesh, in_specs=in_specs, out_specs=out_specs, check_vma=False)
```

```python
import functools
import math

import jax
import jax.numpy as jnp
import ml_dtypes
import numpy as np
from jax import lax
from jax.experimental import pallas as pl
from jax.experimental.pallas import tpu as pltpu
from jax.sharding import PartitionSpec as P

CH = 256
TAPS = 12
SPEC = 512
MESH = pl.DeviceIdType.MESH


def prototype():
    count = TAPS * 2 * CH
    index = jnp.arange(count, dtype=jnp.float32)
    frame = 2.0 * CH
    shifted = (index + 0.5) / frame - TAPS / 2.0
    window = 0.5 - 0.5 * jnp.cos(2.0 * math.pi * (index + 0.5) / count)
    return (jnp.sinc(shifted) * window).astype(jnp.float32).reshape(TAPS, 2 * CH)


def twiddle():
    frame = 2 * CH
    phase = np.arange(CH)[:, None] * np.arange(frame)[None, :] % frame * (2.0 * math.pi / frame)
    table = np.stack([np.cos(phase), -np.sin(phase)], axis=1)
    return table.reshape(2 * CH, frame).astype(np.float32).astype(ml_dtypes.bfloat16)


def tile(rows, cols):
    half = rows.shape[0] // 2
    gram = lax.dot_general(rows, cols, (((1,), (1,)), ((), ())), preferred_element_type=jnp.float32)
    real = gram[:half, :half] + gram[half:, half:]
    imag = gram[half:, :half] - gram[:half, half:]
    return real * (1.0 / SPEC), imag * (1.0 / SPEC)


def correlate_kernel(n, halves, place_keep, place_swap, out, own, xbuf, xsend, xrecv, nbuf, fbuf, ts, tr, nsend, nrecv, frecv, tsend, trecv):
    me = lax.axis_index("blk")
    half, chans, block = n // 2, own.shape[0], own.shape[1] // 2
    mid = half - 1
    side = me // half
    step = 1 - 2 * side
    place = me * step + (n - 1) * side
    inner = {"blk": me + step}

    def pass_near(t, c, src):
        return pltpu.make_async_remote_copy(
            src, nbuf.at[t, c], nsend.at[t, c], nrecv.at[t, c], device_id=inner, device_id_type=MESH)

    def pass_far(t, c, src):
        return pltpu.make_async_remote_copy(
            src, fbuf.at[t, c], nsend.at[t, c], frecv.at[t, c], device_id=inner, device_id_type=MESH)

    def give(t, v, slot, c):
        return pltpu.make_async_remote_copy(
            ts.at[t, v, c], tr.at[slot, c], tsend.at[t, v, c], trecv.at[slot, c],
            device_id={"blk": lax.rem(me - (t + 1) * step + n, n)}, device_id_type=MESH)

    def start(t, c, src):
        @pl.when(place < mid)
        def _():
            pass_near(t, c, src).start()

        @pl.when(place == mid)
        def _():
            pass_far(t, c, src).start()

    def put(c, column, real, imag):
        at = pl.ds(pl.multiple_of(column * block, block), block)
        out[c, 0, :, at] = real.astype(jnp.float32)
        out[c, 1, :, at] = imag.astype(jnp.float32)

    def relay(t, v, slot, c, rows, cols):
        real, imag = tile(rows, cols)
        ts[t, v, c, 0] = real.astype(jnp.bfloat16)
        ts[t, v, c, 1] = imag.astype(jnp.bfloat16)
        give(t, v, slot, c).start()

    group = lax.axis_index("freq")
    z = lax.rem(group // 2, 2)
    partner = {"freq": group + 2 - 4 * z}

    def exchange(c):
        return pltpu.make_async_remote_copy(
            halves.at[1 - z, c], xbuf.at[c], xsend.at[c], xrecv.at[c], device_id=partner, device_id_type=MESH)

    barrier = pltpu.get_barrier_semaphore()
    for k in range(1, n):
        pl.semaphore_signal(barrier, 1, device_id={"blk": lax.rem(me + k, n)}, device_id_type=MESH)
    pl.semaphore_signal(barrier, 1, device_id=partner, device_id_type=MESH)
    pl.semaphore_wait(barrier, n)

    for c in range(chans):
        exchange(c).start()

    @pl.loop(0, chans)
    def _(c):
        exchange(c).wait_recv()
        for p in range(2):
            rows = pl.ds(p * (block // 2), block // 2)
            mixed = jnp.dot(place_keep[...], halves[z, c, rows, :], preferred_element_type=jnp.float32)
            mixed += jnp.dot(place_swap[...], xbuf[c, rows, :], preferred_element_type=jnp.float32)
            own[c, pl.ds(p * block, block), :] = mixed.astype(jnp.bfloat16)
        start(0, c, own.at[c])

    @pl.loop(0, chans)
    def _(c):
        exchange(c).wait_send()
        put(c, me, *tile(own[c], own[c]))

    @pl.loop(0, half)
    def _(t):
        @pl.loop(0, chans)
        def _(c):
            @pl.when(t < place)
            def _():
                pass_near(t, c, own.at[c]).wait_recv()
                start(t + 1, c, nbuf.at[t, c])

            @pl.when(place == mid)
            def _():
                pass_far(t, c, own.at[c]).wait_recv()

            @pl.when(t < place)
            def _():
                relay(t, 0, place, c, nbuf[t, c], own[c])

            @pl.when(place == mid)
            def _():
                @pl.loop(0, mid)
                def _(k):
                    r = mid - 1 - k

                    @pl.when(r <= t)
                    def _():
                        relay(r, 1 + t, half + t, c, nbuf[r, c], fbuf[t, c])

                @pl.when(t < mid)
                def _():
                    @pl.loop(0, mid)
                    def _(u):
                        @pl.when(u < t)
                        def _():
                            relay(t, 1 + u, half + u, c, nbuf[t, c], fbuf[u, c])

                put(c, me + (t + 1) * step, *tile(own[c], fbuf[t, c]))

            @pl.when(t < place)
            def _():
                put(c, me - (t + 1) * step, *tile(own[c], nbuf[t, c]))

    @pl.when(place < mid)
    def _():
        @pl.loop(0, n)
        def _(slot):
            @pl.when(slot > place)
            def _():
                @pl.loop(0, chans)
                def _(c):
                    give(0, 0, slot, c).wait_recv()
                    put(c, me + (slot - place) * step, tr[slot, c, 0], tr[slot, c, 1])

    @pl.loop(0, chans)
    def _(c):
        @pl.loop(0, half)
        def _(t):
            @pl.when(t <= place)
            def _():
                pass_far(t, c, own.at[c]).wait_send()

            @pl.when(t < place)
            def _():
                give(t, 0, 0, c).wait_send()

            @pl.when((place == mid) & (t < mid))
            def _():
                @pl.loop(1, half + 1)
                def _(v):
                    give(t, v, 0, c).wait_send()


def correlate(n, halves, place_keep, place_swap):
    _, chans, block, spec = halves.shape
    half, rows = n // 2, 2 * block
    own = pltpu.VMEM((chans, rows, spec), jnp.bfloat16)
    near = pltpu.VMEM((half - 1, chans, rows, spec), jnp.bfloat16)
    far = pltpu.VMEM((half, chans, rows, spec), jnp.bfloat16)
    leaving = pltpu.VMEM((half - 1, half + 1, chans, 2, block, block), jnp.bfloat16)
    arriving = pltpu.VMEM((n, chans, 2, block, block), jnp.bfloat16)
    dma = pltpu.SemaphoreType.DMA
    return pl.pallas_call(
        functools.partial(correlate_kernel, n),
        out_shape=jax.ShapeDtypeStruct((chans, 2, block, n * block), jnp.float32),
        in_specs=[pl.BlockSpec(memory_space=pltpu.VMEM)] * 3,
        out_specs=pl.BlockSpec(memory_space=pltpu.VMEM),
        scratch_shapes=[
            own, pltpu.VMEM(halves.shape[1:], jnp.bfloat16), dma((chans,)), dma((chans,)),
            near, far, leaving, arriving, dma((half, chans)), dma((half - 1, chans)), dma((half, chans)),
            dma((half - 1, half + 1, chans)), dma((n, chans))],
        compiler_params=pltpu.CompilerParams(
            collective_id=0, has_side_effects=True, vmem_limit_bytes=48 << 20),
    )(halves, place_keep, place_swap)


def body(n, samples, slot_order, flags):
    inputs = samples.shape[0]
    taps = prototype()
    table = jnp.asarray(twiddle())
    good = (1 - flags).astype(jnp.float32)
    frames = samples.reshape(inputs, SPEC + TAPS - 1, 2 * CH)
    total = jnp.zeros((inputs, SPEC, 2 * CH), jnp.float32)
    for tap in range(TAPS):
        total = total + taps[tap][None, None, :] * frames[:, tap : tap + SPEC, :].astype(jnp.float32)
    fir = total.astype(jnp.bfloat16)
    spectra = jnp.einsum("kn,isn->iks", table, fir, preferred_element_type=jnp.float32)
    squares = jnp.sum(spectra * spectra, axis=2)
    power = jnp.sum(squares.reshape(inputs, CH, 2), axis=2) / SPEC
    scale = good[:, None] / jnp.sqrt(power + 1e-05)
    quantized = (spectra * jnp.repeat(scale, 2, axis=1)[:, :, None]).astype(jnp.bfloat16)

    groups = lax.axis_size("freq")
    rows, columns = 2 * CH // groups, groups // 4
    plane = [[f for f in range(groups) if f // 2 % 2 == z] for z in range(2)]
    leaving = quantized.reshape(inputs, columns, 2, 2, rows, SPEC).transpose(1, 3, 2, 0, 4, 5)
    arrived = lax.all_to_all(
        leaving.reshape(2 * columns, 2 * inputs * rows, SPEC), "freq", 0, 0, axis_index_groups=plane, tiled=True)
    held = 2 * columns * inputs
    halves = arrived.reshape(2 * columns, 2, inputs, rows, SPEC).transpose(1, 3, 2, 0, 4)
    halves = halves.reshape(2, rows // 2, 2 * held, SPEC)
    z = lax.axis_index("freq") // 2 % 2
    wanted = slot_order[0]
    chip = 2 * inputs
    source = wanted // (2 * chip) * 2 + wanted % chip // inputs
    inside = wanted % inputs * (2 * columns) + source
    onehot = inside[:, None] == jnp.arange(held)[None, :]
    here = (wanted // chip % 2 == z)[:, None]
    return correlate(
        n, halves, (onehot & here).astype(jnp.bfloat16), (onehot & ~here).astype(jnp.bfloat16))


def solution(mesh):
    in_specs = (P(("blk", "freq"), None), P("blk", None), P(("blk", "freq")))
    out_specs = P("freq", None, "blk", None)
    return jax.shard_map(
        functools.partial(body, mesh.shape["blk"]), mesh=mesh, in_specs=in_specs, out_specs=out_specs, check_vma=False)
```
